32 devices in a mesh: clip: 4 (over z), band: 4 (over x, core), chan: 2 (over y).
Axes of the slice: x: 2, y: 2, z: 4, core: 2. Of those that a mesh axis runs over, the one named last changes fastest.
Arguments:
- frames: bfloat16 [512, 4, 5120], P(None, 'clip', ('band', 'chan')), may hold values from -6 to 6
- weight: bfloat16 [512, 3, 3, 512], P('chan'), may hold values from -0.09375 to 0.09375
- bias: float32 [512], replicated, may hold values from -3 to 3
- cotangent: bfloat16 [512, 4, 5120], P(None, 'clip', ('band', 'chan')), may hold values from -6 to 6
Outputs:
- outputs: bfloat16 [512, 4, 5120], P(None, 'clip', ('band', 'chan'))
- grad_frames: bfloat16 [512, 4, 5120], P(None, 'clip', ('band', 'chan'))
- grad_weight: float32 [512, 3, 3, 512], P('chan')
- grad_bias: float32 [512], P('chan')
The draws below stay inside these ranges and needn't reach their ends.
All inputs are finite; a program needn't handle non-finite values.
Results may differ from the reference program's by a relative error of at most 0.001.
Values may be sent and summed in bfloat16 or wider, within the bound.
A program may use at most 128 MiB of HBM per device.

```python
import math
import jax
import jax.numpy as jnp
from jax import lax

C = 512
W = 160
H = 32
FRAMES = 4


def block_scale(stream_key, dims, cuts, smallest, top_value):
    gain = 1.0
    for dim, parts in cuts:
        steps = jax.random.uniform(jax.random.fold_in(jax.random.fold_in(stream_key, 6), dim), (parts,), jnp.float32, smallest / len(cuts), top_value / len(cuts))
        gain = gain * jnp.repeat(jnp.exp(steps), dims[dim] // parts).reshape((-1,) + (1,) * (len(dims) - 1 - dim))
    return gain


def normal_values(stream_key, dims, deviation, limit, shards=(), kind=jnp.bfloat16):
    values = deviation * jax.random.normal(stream_key, dims, jnp.float32)
    if shards:
        values = values * block_scale(stream_key, dims, shards, -0.22, 0.18)
    return jnp.clip(values, -limit, limit).astype(kind)


def setup_inputs(seed: int = 0) -> dict:
    splits = jax.random.split(jax.random.key(seed), 5)
    return {
        "frames": normal_values(splits[0], (C, FRAMES, H * W), 1.0, 6.0, ((1, 4), (2, 8))),
        "weight": normal_values(splits[1], (C, 3, 3, C), (9 * C) ** -0.5, 0.09375, ((0, 2),)),
        "bias": normal_values(splits[2], (C,), 0.5, 3.0, (), jnp.float32),
        "cotangent": normal_values(splits[3], (C, FRAMES, H * W), 1.0, 6.0, ((1, 4), (2, 8))),
    }


def reference(frames, weight, bias, cotangent):
    channels, frame_count, cell_total = frames.shape
    row_count = cell_total // W
    inputs = frames.astype(jnp.float32).reshape(channels, frame_count, row_count, W)
    kernel = weight.astype(jnp.float32)
    upstream = cotangent.astype(jnp.float32).reshape(channels, frame_count, row_count, W)
    margin = ((0, 0), (0, 0), (1, 1), (1, 1))
    padded_in = jnp.pad(inputs, margin)
    padded_cot = jnp.pad(upstream, margin)
    scale = 1.0 / math.sqrt(frame_count * row_count * W)
    running = jnp.zeros(inputs.shape, jnp.float32) + bias[:, None, None, None]
    grad_in = jnp.zeros(inputs.shape, jnp.float32)
    tap_rows = []
    for a in range(3):
        tap_row = []
        for b in range(3):
            window = padded_in[:, :, a:a + row_count, b:b + W]
            running = running + jnp.einsum('ifhw,oi->ofhw', window, kernel[:, a, b, :])
            back = padded_cot[:, :, 2 - a:2 - a + row_count, 2 - b:2 - b + W]
            grad_in = grad_in + jnp.einsum('ofhw,oi->ifhw', back, kernel[:, a, b, :])
            tap_row.append(jnp.einsum('ifhw,ofhw->oi', window, upstream))
        tap_rows.append(jnp.stack(tap_row, axis=1))
    grad_weight = jnp.stack(tap_rows, axis=1) * scale
    grad_bias = lax.optimization_barrier(jnp.sum(upstream, axis=(1, 2, 3))) * scale
    outputs = running.reshape(channels, frame_count, cell_total).astype(jnp.bfloat16)
    grad_frames = grad_in.reshape(channels, frame_count, cell_total).astype(jnp.bfloat16)
    return (outputs, grad_frames, grad_weight, grad_bias)
```

```python
import functools
import math

import jax
import jax.numpy as jnp
from jax import lax
from jax.experimental import pallas as pl
from jax.experimental.pallas import tpu as pltpu
from jax.sharding import PartitionSpec as P

W = 160
MESH = pl.DeviceIdType.MESH
F32 = jnp.float32
BF16 = jnp.bfloat16


def ds(start, size):
    return pl.ds(pl.multiple_of(start, size), size)


def remote(src, dst, send, recv, device):
    return pltpu.make_async_remote_copy(
        src_ref=src, dst_ref=dst, send_sem=send, recv_sem=recv, device_id=device, device_id_type=MESH
    )


def sides(rows):
    wide = rows.astype(F32)
    at = lax.broadcasted_iota(jnp.int32, wide.shape, 0)
    left = jnp.where(at == 0, 0.0, pltpu.roll(wide, 1, 0)).astype(BF16)
    right = jnp.where(at == W - 1, 0.0, pltpu.roll(wide, W - 1, 0)).astype(BF16)
    return left, rows, right


def encode(dst, at, value):
    rows, lanes = value.shape
    wide = value.reshape(rows // 16, 16, lanes)
    top = jnp.maximum(jnp.max(jnp.abs(wide), axis=0), 1e-35).astype(BF16)
    u = wide * (1.0 / top.astype(F32))
    power = u * u
    power = power * power
    power = power * power
    code = jnp.where(u < 0.0, -power, power).reshape(rows, lanes)
    dst[(*at, pl.ds(0, 16), slice(None))] = top
    dst[(*at, pl.ds(16, rows), slice(None))] = code.astype(BF16)


def decode(block):
    rows, lanes = block.shape
    top = block[:16].astype(F32)
    code = block[16:].astype(F32)
    root = jnp.exp(jnp.log(jnp.abs(code)) * 0.125)
    root = jnp.where(code > 0.0, root, jnp.where(code < 0.0, -root, 0.0))
    return (root.reshape(rows // 16 - 1, 16, lanes) * top).reshape(rows - 16, lanes)


def kernel(
    dims, x_in, g_in, w_ref, bias_in, o_ref, db_ref, out_ref, back_ref,
    xs, gs, dx, xe, ge, kern, acc, share, coded, got1, got2, dbs, dgot, hx, hg, xt_ref, gt_ref, x_ref, g_ref, bias_ref, sems, regs,
):
    clips, bands, chans, rows_o, rows_i, cells, channels, scale = dims
    group = bands * chans
    half = rows_o // 2
    lanes = channels // clips
    width = bands // 2
    units = cells // W
    total = cells * group
    z, b, n = lax.axis_index("clip"), lax.axis_index("band"), lax.axis_index("chan")
    me = b * chans + n
    core = b % 2
    sib = b + 1 - 2 * core
    sib_id = {"band": sib}
    nxt, prv = (me + 1) % group, (me + group - 1) % group
    nxt_id = {"band": nxt // chans, "chan": nxt % chans}
    prv_id = {"band": prv // chans, "chan": prv % chans}
    z0 = z % 2
    inner = (z + 1) // 2 == 1
    near, middle = {"clip": z + 1 - 2 * z0}, {"clip": clips - 1 - z}

    loads = [
        pltpu.make_async_copy(src, dst, regs.at[3 + i])
        for i, (src, dst) in enumerate(((x_in, x_ref), (g_in, g_ref), (bias_in, bias_ref)))
    ]
    for load in loads:
        load.start()
    barrier = pltpu.get_barrier_semaphore()
    targets = [{"clip": (z + k) % clips} for k in range(1, clips)]
    for k in range(1, group):
        to = (me + k) % group
        targets.append({"band": to // chans, "chan": to % chans})
    for target in targets:
        pl.semaphore_signal(barrier, inc=1, device_id=target, device_id_type=MESH)

    def turn(src, dst):
        @pl.loop(0, cells // 128)
        def _(t):
            dst[ds(t * 128, 128), :] = src[:, ds(t * 128, 128)].astype(F32).T.astype(BF16)

    loads[0].wait()
    turn(x_ref, xt_ref)
    loads[1].wait()
    loads[2].wait()
    pl.semaphore_wait(barrier, len(targets))

    started = []
    names = {}

    def pair(key):
        if key not in names:
            names[key] = len(names)
        return sems.at[0, names[key]], sems.at[1, names[key]]

    def send(src, dst, key, device):
        s, r = pair(key)
        copy = remote(src, dst, s, r, device)
        copy.start()
        started.append(copy)

    def arrive(dst, key):
        s, r = pair(key)
        remote(dst, dst, s, r, sib_id).wait_recv()

    def slab(src_n, part, zz):
        return kern.at[:, ds((2 * src_n + part) * half, half), ds(zz * lanes, lanes)]

    keep_w = pltpu.make_async_copy(w_ref, kern.at[:, ds(n * rows_o, rows_o), :], regs.at[0])
    keep_x = pltpu.make_async_copy(xt_ref.at[:, ds(b * rows_i, rows_i)], xs.at[ds(me * cells, cells), :], regs.at[1])
    keep_g = pltpu.make_async_copy(g_ref.at[ds(n * rows_o, rows_o), :], gs.at[:, ds(me * cells, cells)], regs.at[2])

    def x_place(src_b, src_n):
        return xs.at[ds((src_b * chans + src_n) * cells, cells), :]

    def g_place(src_b, src_n):
        return gs.at[:, ds((src_b * chans + src_n) * cells, cells)]

    for m in range(1, chans):
        send(w_ref.at[:, ds(core * half, half), ds(z * lanes, lanes)], slab(n, core, z), ("w", m), {"chan": (n + m) % chans})
    for d in range(1, bands):
        to_b = (b + d) % bands
        send(xt_ref.at[:, ds(to_b * rows_i, rows_i)], x_place(b, n), ("x", d, 0), {"band": to_b})
    for m in range(1, chans):
        to_n = (n + m) % chans
        send(g_ref.at[ds(to_n * rows_o, rows_o), :], g_place(b, n), ("g", 0, m), {"chan": to_n})
        send(xt_ref.at[:, ds(b * rows_i, rows_i)], x_place(b, n), ("x", 0, m), {"chan": to_n})
    own_g = g_ref.at[ds(n * rows_o, rows_o), :]
    for j in range(1, width):
        send(own_g, g_place(b, n), ("g", j, 0), {"band": (b + 2 * j) % bands})
    send(own_g, g_place(b, n), ("f", 0, 0), sib_id)
    keep_x.start()
    keep_g.start()
    keep_w.start()

    def widen(dst, to, rows, size):
        for t, part in enumerate(sides(rows)):
            dst[ds(to, W), t * size:(t + 1) * size] = part

    def widen_block(src):
        @pl.loop(0, units)
        def _(u):
            at = src * cells + u * W
            widen(dx, at + W, xs[ds(at, W), :], rows_i)

    for m in range(1, chans):
        src = (n + chans - m) % chans
        arrive(slab(src, core, z), ("w", m))
        for q in range(1, clips):
            send(slab(src, core, z), slab(src, core, z), ("wz", m, q), {"clip": (z + q) % clips})
        send(slab(src, core, z), slab(src, core, z), ("ws", m, 0), sib_id)
    for d in range(1, bands):
        place = x_place((b + bands - d) % bands, n)
        arrive(place, ("x", d, 0))
        for m in range(1, chans):
            send(place, place, ("x", d, m), {"chan": (n + m) % chans})
    for m in range(1, chans):
        place = g_place(b, (n + chans - m) % chans)
        arrive(place, ("g", 0, m))
        for j in range(1, width):
            send(place, place, ("g", j, m), {"band": (b + 2 * j) % bands})
        send(place, place, ("f", 0, m), sib_id)
    for j in range(1, width):
        place = g_place((b + bands - 2 * j) % bands, n)
        arrive(place, ("g", j, 0))
        send(place, place, ("f", j, 0), sib_id)

    turn(g_ref, gt_ref)
    dx[pl.ds(0, W), :] = jnp.zeros((W, 3 * rows_i), BF16)
    dx[pl.ds(total + W, W), :] = jnp.zeros((W, 3 * rows_i), BF16)

    @pl.loop(0, units)
    def _(u):
        widen(xe, (u + 1) * W, xt_ref[ds(u * W, W), :], channels)
        widen(ge, (u + 1) * W, gt_ref[ds(u * W, W), :], channels)

    keep_x.wait()
    widen_block(me)
    for d in range(1, bands):
        widen_block(((b + bands - d) % bands) * chans + n)
    for m in range(1, chans):
        src_n = (n + chans - m) % chans
        arrive(x_place(b, src_n), ("x", 0, m))
        widen_block(b * chans + src_n)
    for j in range(1, width):
        for m in range(1, chans):
            place = g_place((b + bands - 2 * j) % bands, (n + chans - m) % chans)
            arrive(place, ("g", j, m))
            send(place, place, ("f", j, m), sib_id)
    for d in range(1, bands):
        for m in range(1, chans):
            src_b, src_n = (b + bands - d) % bands, (n + chans - m) % chans
            arrive(x_place(src_b, src_n), ("x", d, m))
            widen_block(src_b * chans + src_n)
    send(xt_ref.at[pl.ds(cells - W, W), :], hx.at[0], ("hx", 0), nxt_id)
    send(gt_ref.at[pl.ds(cells - W, W), :], hg.at[0], ("hg", 0), nxt_id)
    send(xt_ref.at[pl.ds(0, W), :], hx.at[1], ("hx", 1), prv_id)
    send(gt_ref.at[pl.ds(0, W), :], hg.at[1], ("hg", 1), prv_id)
    for j in range(width):
        for m in range(chans):
            arrive(g_place((sib + bands - 2 * j) % bands, (n + chans - m) % chans), ("f", j, m))
    keep_g.wait()

    block = 2 * cells

    def tap_row(a):
        acc2 = acc.at[pl.ds(0, rows_o), pl.ds(0, 3 * rows_i)]
        acc2[...] = jnp.zeros((rows_o, 3 * rows_i), F32)

        @pl.loop(0, group // 2)
        def _(k):
            rows = pl.ds(pl.multiple_of(k * block + a * W, 32), block)
            acc2[...] += jnp.dot(gs[:, ds(k * block, block)], dx[rows, :], preferred_element_type=F32)

        for t in range(3):
            share[3 * a + t] = acc2[:, t * rows_i:(t + 1) * rows_i] * scale

    side = z // 2

    def spot(t, part, bb):
        return o_ref.at[t, part, :, ds(bb * rows_i, rows_i)]

    def spread(t, part, step):
        place = spot(t, part, b)
        for j in range(1, width):
            send(place, place, ("xo", t, step, j), {"band": (b + 2 * j) % bands})
        send(place, place, ("c", t, step, 0), sib_id)

    def give(t):
        for part in range(2):
            encode(coded, (t, part), share[t, part * half:(part + 1) * half, :])
        send(coded.at[t], got1.at[t], ("r1", t), near)

    def take(t):
        arrive(got1.at[t], ("r1", t))
        for part in range(2):
            share[t, part * half:(part + 1) * half, :] += decode(got1[t, part])
        encode(coded, (t, 0), share[t, ds((1 - side) * half, half), :])
        send(coded.at[t, 0], got2.at[t], ("r2", t), middle)

    def settle(t):
        arrive(got2.at[t], ("r2", t))
        encode(coded, (t, 1), share[t, ds(side * half, half), :] + decode(got2[t]))
        place = spot(t, side, b)
        place[...] = coded[t, 1]
        send(coded.at[t, 1], place, ("a1", t), middle)
        send(coded.at[t, 1], place, ("a2", t, 0), near)
        spread(t, side, 0)

    def share_back(t):
        place = spot(t, 1 - side, b)
        arrive(place, ("a1", t))
        send(place, place, ("a2", t, 1), near)
        spread(t, 1 - side, 1)

    def receive(t):
        for step, part in enumerate((side, 1 - side)):
            arrive(spot(t, part, b), ("a2", t, step))
            spread(t, part, step)

    def cross(t):
        for step, part in enumerate((side, 1 - side)):
            for j in range(1, width):
                place = spot(t, part, (b + bands - 2 * j) % bands)
                arrive(place, ("xo", t, step, j))
                send(place, place, ("c", t, step, j), sib_id)

    def finish(t):
        for step, part in enumerate((side, 1 - side)):
            for j in range(width):
                arrive(spot(t, part, (sib + bands - 2 * j) % bands), ("c", t, step, j))

    def conv(a):
        @pl.loop(0, channels // 256)
        def _(t):
            rows = ds(t * 256, 256)
            if a == 0:
                column = jnp.broadcast_to(bias_ref[:, rows], (8, 256)).T[:, :1]
                part = jnp.zeros((256, cells), F32) + column
            else:
                part = acc[rows, :]
            for s in range(3):
                part += lax.dot_general(
                    kern[3 * a + s, rows, :], xe[a * W:a * W + cells, s * channels:(s + 1) * channels],
                    (((1,), (1,)), ((), ())), preferred_element_type=F32,
                )
            if a == 2:
                out_ref[rows, :] = part.astype(BF16)
            else:
                acc[rows, :] = part

    half_cells = cells // 2

    def back(a):
        @pl.loop(0, 2)
        def _(t):
            rows = ds(t * half_cells, half_cells)
            c = 2 - a
            part = jnp.zeros((half_cells, channels), F32)
            if a:
                part = acc[ds(t * half_cells, half_cells), pl.ds(0, channels)]
            for s in range(3):
                part += jnp.dot(
                    ge[pl.ds(pl.multiple_of(c * W + t * half_cells, 32), half_cells), (2 - s) * channels:(3 - s) * channels],
                    kern[3 * a + s], preferred_element_type=F32,
                )
            acc[rows, pl.ds(0, channels)] = part

        if a == 2:
            @pl.loop(0, cells // 128)
            def _(t):
                back_ref[:, ds(t * 128, 128)] = acc[ds(t * 128, 128), pl.ds(0, channels)].T.astype(BF16)

    def bias_sum():
        ones = jnp.ones((8, block), BF16)
        dbs[...] = jnp.zeros((8, rows_o), F32)

        @pl.loop(0, group // 2)
        def _(k):
            dbs[...] += lax.dot_general(
                ones, gs[:, ds(k * block, block)], (((1,), (1,)), ((), ())), preferred_element_type=F32
            )

        for q in range(1, clips):
            send(dbs, dgot.at[q], ("d", q), {"clip": (z + q) % clips})

    def halos():
        for h in range(2):
            arrive(hx.at[h], ("hx", h))
            arrive(hg.at[h], ("hg", h))
            edge = me == (0 if h == 0 else group - 1)
            for src, dst in ((hx, xe), (hg, ge)):
                rows = src[h]
                rows = jnp.where(edge, jnp.zeros_like(rows), rows)
                for t, part in enumerate(sides(rows)):
                    dst[pl.ds(h * (cells + W), W), t * channels:(t + 1) * channels] = part

    def weights():
        for m in range(1, chans):
            src = (n + chans - m) % chans
            for q in range(1, clips):
                zz = (z + clips - q) % clips
                arrive(slab(src, core, zz), ("wz", m, q))
                send(slab(src, core, zz), slab(src, core, zz), ("ws", m, q), sib_id)
        for m in range(1, chans):
            src = (n + chans - m) % chans
            for q in range(clips):
                arrive(slab(src, 1 - core, (z + clips - q) % clips), ("ws", m, q))
        keep_w.wait()

    def matmuls():
        yield halos()
        yield weights()
        for a in range(3):
            yield conv(a)
        for a in range(3):
            yield back(a)

    gathered = list(started)

    def second_half(role):
        started.clear()
        work = matmuls()
        for a in range(3):
            tap_row(a)
            if not role:
                for t in range(3 * a, 3 * a + 3):
                    give(t)
        bias_sum()
        if role:
            for t in range(13):
                for step, lag in ((take, 0), (settle, 1), (share_back, 2), (cross, 4)):
                    if 0 <= t - lag < 9:
                        step(t - lag)
                if t >= 3:
                    next(work, None)
        else:
            for t in range(11):
                for step, lag in ((receive, 0), (cross, 2)):
                    if 0 <= t - lag < 9:
                        step(t - lag)
                if t >= 2:
                    next(work, None)
        for _ in work:
            pass
        for q in range(1, clips):
            arrive(dgot.at[q], ("d", q))
        sums = dbs[...]
        for q in range(1, clips):
            sums = sums + dgot[q]
        db_ref[...] = sums[:1] * scale
        for t in range(9):
            finish(t)
        for copy in started:
            copy.wait_send()

    @pl.when(inner)
    def _():
        second_half(True)

    @pl.when(jnp.logical_not(inner))
    def _():
        second_half(False)

    for copy in gathered:
        copy.wait_send()


def emit(*refs):
    sources, places, wide, sems = refs[:4], refs[4:8], refs[8], refs[9]
    copies = [pltpu.make_async_copy(src, dst, sems.at[i]) for i, (src, dst) in enumerate(zip(sources[1:], places[1:]))]
    for copy in copies:
        copy.start()
    taps, parts, rows, _ = sources[0].shape
    rows -= 16

    def out(t):
        return pltpu.make_async_copy(wide.at[t], places[0].at[t], sems.at[3 + t])

    @pl.loop(0, taps)
    def _(t):
        for part in range(parts):
            wide[t, part * rows:(part + 1) * rows, :] = decode(sources[0][t, part])
        out(t).start()

    @pl.loop(0, taps)
    def _(t):
        out(t).wait()

    for copy in copies:
        copy.wait()


VM = pl.BlockSpec(memory_space=pltpu.VMEM)


def local(frames, weight, bias, cotangent):
    channels, frame_count, cells = frames.shape
    clips, bands, chans = (lax.axis_size(a) for a in ("clip", "band", "chan"))
    group = bands * chans
    assert frame_count == 1 and cells % W == 0 and clips == 4
    total = cells * group
    scale = 1.0 / math.sqrt(frame_count * clips * total)
    rows_i, rows_o = channels // bands, channels // chans
    x = frames.reshape(channels, cells)
    g = cotangent.reshape(channels, cells)
    wt = jnp.transpose(weight, (1, 2, 0, 3)).reshape(9, rows_o, channels)
    half = rows_o // 2
    width = bands // 2
    copies = (chans - 1) * (1 + clips - 1 + clips) + 2 * width * chans + group + bands * chans + 4 + clips + 9 * (5 + 4 * width) + 8
    limit = (24 << 20) + (total + 2 * W) * 4 * rows_i * 2 + rows_o * total * 2 + rows_o * channels * 72
    shape = jax.ShapeDtypeStruct
    result = pltpu.VMEM if limit < (50 << 20) else shape
    grad, db, outputs, back = pl.pallas_call(
        functools.partial(kernel, (clips, bands, chans, rows_o, rows_i, cells, channels, scale)),
        out_shape=(
            result((9, 2, half + 16, channels), BF16),
            result((1, rows_o), F32),
            result((channels, cells), BF16),
            result((channels, cells), BF16),
        ),
        in_specs=[pl.BlockSpec(memory_space=pltpu.HBM)] * 4,
        out_specs=(VM,) * 4,
        scratch_shapes=[
            pltpu.VMEM((total, rows_i), BF16),
            pltpu.VMEM((rows_o, total), BF16),
            pltpu.VMEM((total + 2 * W, 3 * rows_i), BF16),
            pltpu.VMEM((cells + 2 * W, 3 * channels), BF16),
            pltpu.VMEM((cells + 2 * W, 3 * channels), BF16),
            pltpu.VMEM((9, channels, channels), BF16),
            pltpu.VMEM((max(channels, cells), max(channels, cells)), F32),
            pltpu.VMEM((9, rows_o, rows_i), F32),
            pltpu.VMEM((9, 2, half + 16, rows_i), BF16),
            pltpu.VMEM((9, 2, half + 16, rows_i), BF16),
            pltpu.VMEM((9, half + 16, rows_i), BF16),
            pltpu.VMEM((8, rows_o), F32),
            pltpu.VMEM((clips, 8, rows_o), F32),
            pltpu.VMEM((2, W, channels), BF16),
            pltpu.VMEM((2, W, channels), BF16),
            pltpu.VMEM((cells, channels), BF16),
            pltpu.VMEM((cells, channels), BF16),
            pltpu.VMEM((channels, cells), BF16),
            pltpu.VMEM((channels, cells), BF16),
            pltpu.VMEM((1, channels), F32),
            pltpu.SemaphoreType.DMA((2, copies)),
            pltpu.SemaphoreType.DMA((6,)),
        ],
        compiler_params=pltpu.CompilerParams(collective_id=0, has_side_effects=True, vmem_limit_bytes=min(67000000, limit)),
    )(*(pltpu.with_memory_space_constraint(v, pltpu.HBM) for v in (x, g, wt, bias[None, :])))
    results = (grad, db, outputs, back)
    grad, db, outputs, back = pl.pallas_call(
        emit,
        out_shape=(shape((9, rows_o, channels), F32),) + tuple(shape(r.shape, r.dtype) for r in results[1:]),
        in_specs=[VM] * 4,
        out_specs=(pl.BlockSpec(memory_space=pl.ANY),) * 4,
        scratch_shapes=[pltpu.VMEM((9, rows_o, channels), F32), pltpu.SemaphoreType.DMA((12,))],
        compiler_params=pltpu.CompilerParams(vmem_limit_bytes=16 << 20),
    )(*results)
    outputs = outputs.reshape(frames.shape)
    grad_frames = back.reshape(frames.shape)
    grad_weight = jnp.transpose(grad.reshape(3, 3, rows_o, channels), (2, 0, 1, 3))
    return outputs, grad_frames, grad_weight, db[0]


def solution(mesh):
    cells = P(None, "clip", ("band", "chan"))
    taps = P("chan", None, None, None)
    return jax.shard_map(
        local, mesh=mesh, in_specs=(cells, taps, P(), cells), out_specs=(cells, cells, taps, P("chan")), check_vma=False
    )
```

```python
import functools
import math

import jax
import jax.numpy as jnp
from jax import lax
from jax.experimental import pallas as pl
from jax.experimental.pallas import tpu as pltpu
from jax.sharding import PartitionSpec as P

W = 160
MESH = pl.DeviceIdType.MESH
F32 = jnp.float32
BF16 = jnp.bfloat16


def ds(start, size):
    return pl.ds(pl.multiple_of(start, size), size)


def remote(src, dst, send, recv, device):
    return pltpu.make_async_remote_copy(
        src_ref=src, dst_ref=dst, send_sem=send, recv_sem=recv, device_id=device, device_id_type=MESH
    )


def sides(rows):
    wide = rows.astype(F32)
    at = lax.broadcasted_iota(jnp.int32, wide.shape, 0)
    left = jnp.where(at == 0, 0.0, pltpu.roll(wide, 1, 0)).astype(BF16)
    right = jnp.where(at == W - 1, 0.0, pltpu.roll(wide, W - 1, 0)).astype(BF16)
    return left, rows, right


def encode(dst, at, value):
    rows, lanes = value.shape
    wide = value.reshape(rows // 16, 16, lanes)
    top = jnp.maximum(jnp.max(jnp.abs(wide), axis=0), 1e-35).astype(BF16)
    u = wide * (1.0 / top.astype(F32))
    power = u * u
    power = power * power
    power = power * power
    code = jnp.where(u < 0.0, -power, power).reshape(rows, lanes)
    dst[(*at, pl.ds(0, 16), slice(None))] = top
    dst[(*at, pl.ds(16, rows), slice(None))] = code.astype(BF16)


def decode(block):
    rows, lanes = block.shape
    top = block[:16].astype(F32)
    code = block[16:].astype(F32)
    root = jnp.exp(jnp.log(jnp.abs(code)) * 0.125)
    root = jnp.where(code > 0.0, root, jnp.where(code < 0.0, -root, 0.0))
    return (root.reshape(rows // 16 - 1, 16, lanes) * top).reshape(rows - 16, lanes)


def kernel(
    dims, x_in, g_in, w_ref, bias_in, o_ref, db_ref, out_ref, back_ref,
    xs, gs, dx, xe, ge, kern, acc_f, acc_b, share, coded, got1, got2, dbs, dgot, hx, hg, xt_ref, gt_ref, x_ref, g_ref, bias_ref, sems, regs,
):
    clips, bands, chans, rows_o, rows_i, cells, channels, scale = dims
    group = bands * chans
    half = rows_o // 2
    lanes = channels // clips
    width = bands // 2
    units = cells // W
    split = chans == 2 and rows_o % 256 == 0
    cut = -(-W // 128) * 128
    total = cells * group
    z, b, n = lax.axis_index("clip"), lax.axis_index("band"), lax.axis_index("chan")
    me = b * chans + n
    core = b % 2
    sib = b + 1 - 2 * core
    sib_id = {"band": sib}
    nxt, prv = (me + 1) % group, (me + group - 1) % group
    nxt_id = {"band": nxt // chans, "chan": nxt % chans}
    prv_id = {"band": prv // chans, "chan": prv % chans}
    z0 = z % 2
    inner = (z + 1) // 2 == 1
    near, middle = {"clip": z + 1 - 2 * z0}, {"clip": clips - 1 - z}

    loads = [
        pltpu.make_async_copy(src, dst, regs.at[3 + i])
        for i, (src, dst) in enumerate(((x_in, x_ref), (g_in, g_ref), (bias_in, bias_ref)))
    ]
    for load in loads:
        load.start()
    barrier = pltpu.get_barrier_semaphore()
    targets = [{"clip": (z + k) % clips} for k in range(1, clips)]
    for k in range(1, group):
        to = (me + k) % group
        targets.append({"band": to // chans, "chan": to % chans})
    for target in targets:
        pl.semaphore_signal(barrier, inc=1, device_id=target, device_id_type=MESH)

    def turn(src, dst):
        @pl.loop(0, cells // 128)
        def _(t):
            dst[ds(t * 128, 128), :] = src[:, ds(t * 128, 128)].astype(F32).T.astype(BF16)

    loads[0].wait()
    turn(x_ref, xt_ref)
    loads[1].wait()
    loads[2].wait()
    pl.semaphore_wait(barrier, len(targets))

    started = []
    names = {}

    def pair(key):
        if key not in names:
            names[key] = len(names)
        return sems.at[0, names[key]], sems.at[1, names[key]]

    def send(src, dst, key, device):
        s, r = pair(key)
        copy = remote(src, dst, s, r, device)
        copy.start()
        started.append(copy)

    def arrive(dst, key):
        s, r = pair(key)
        remote(dst, dst, s, r, sib_id).wait_recv()

    def slab(src_n, part, zz):
        return kern.at[:, ds((2 * src_n + part) * half, half), ds(zz * lanes, lanes)]

    keep_w = pltpu.make_async_copy(w_ref, kern.at[:, ds(n * rows_o, rows_o), :], regs.at[0])
    keep_x = pltpu.make_async_copy(xt_ref.at[:, ds(b * rows_i, rows_i)], xs.at[ds(me * cells, cells), :], regs.at[1])
    keep_g = pltpu.make_async_copy(g_ref.at[ds(n * rows_o, rows_o), :], gs.at[:, ds(me * cells, cells)], regs.at[2])

    def x_place(src_b, src_n):
        return xs.at[ds((src_b * chans + src_n) * cells, cells), :]

    def g_place(src_b, src_n):
        return gs.at[:, ds((src_b * chans + src_n) * cells, cells)]

    for m in range(1, chans):
        send(w_ref.at[:, ds(core * half, half), ds(z * lanes, lanes)], slab(n, core, z), ("w", m), {"chan": (n + m) % chans})
    for d in range(1, bands):
        to_b = (b + d) % bands
        send(xt_ref.at[:, ds(to_b * rows_i, rows_i)], x_place(b, n), ("x", d, 0), {"band": to_b})
    for m in range(1, chans):
        to_n = (n + m) % chans
        send(g_ref.at[ds(to_n * rows_o, rows_o), :], g_place(b, n), ("g", 0, m), {"chan": to_n})
        send(xt_ref.at[:, ds(b * rows_i, rows_i)], x_place(b, n), ("x", 0, m), {"chan": to_n})
    own_g = g_ref.at[ds(n * rows_o, rows_o), :]
    for j in range(1, width):
        send(own_g, g_place(b, n), ("g", j, 0), {"band": (b + 2 * j) % bands})
    send(own_g, g_place(b, n), ("f", 0, 0), sib_id)
    keep_x.start()
    keep_g.start()
    keep_w.start()

    def widen(dst, to, rows, size):
        for t, part in enumerate(sides(rows)):
            dst[ds(to, W), t * size:(t + 1) * size] = part

    def widen_block(src):
        @pl.loop(0, units)
        def _(u):
            at = src * cells + u * W
            widen(dx, at + W, xs[ds(at, W), :], rows_i)

    def conv_part(start, count, lo, hi, taps, seed, last):
        @pl.loop(0, count)
        def _(t):
            at, rows = ds(t * 256, 256), ds(start + t * 256, 256)
            if seed:
                part = acc_f[at, lo:hi]
            else:
                column = jnp.broadcast_to(bias_ref[:, rows], (8, 256)).T[:, :1]
                part = jnp.zeros((256, hi - lo), F32) + column
            for a in taps:
                for s in range(3):
                    part += lax.dot_general(
                        kern[3 * a + s, rows, :], xe[a * W + lo:a * W + hi, s * channels:(s + 1) * channels],
                        (((1,), (1,)), ((), ())), preferred_element_type=F32,
                    )
            if last:
                out_ref[rows, lo:hi] = part.astype(BF16)
            else:
                acc_f[at, lo:hi] = part

    def back_part(start, size, lo, hi, rows, seed):
        part = acc_b[lo:hi, :] if seed else jnp.zeros((hi - lo, channels), F32)
        for c in rows:
            for s in range(3):
                cols = pl.ds(pl.multiple_of((2 - s) * channels + start, 128), size)
                part += jnp.dot(
                    ge[c * W + lo:c * W + hi, cols], kern[3 * (2 - c) + s, pl.ds(pl.multiple_of(start, 16), size), :],
                    preferred_element_type=F32,
                )
        acc_b[lo:hi, :] = part

    own, other, stripe = n * rows_o, (1 - n) * rows_o, rows_o // 256

    def conv_early():
        if split:
            keep_w.wait()
            conv_part(own, stripe, 0, cut, (1, 2), False, False)
            conv_part(own, stripe, cut, cells - cut, (0, 1, 2), False, True)
            conv_part(own, stripe, cells - cut, cells, (0, 1), False, False)

    def back_early():
        if split:
            back_part(own, rows_o, 0, W, (1, 2), False)
            back_part(own, rows_o, W, cells - W, (0, 1, 2), False)
            back_part(own, rows_o, cells - W, cells, (0, 1), False)

    turn(g_ref, gt_ref)
    dx[pl.ds(0, W), :] = jnp.zeros((W, 3 * rows_i), BF16)
    dx[pl.ds(total + W, W), :] = jnp.zeros((W, 3 * rows_i), BF16)

    @pl.loop(0, units)
    def _(u):
        widen(xe, (u + 1) * W, xt_ref[ds(u * W, W), :], channels)
        widen(ge, (u + 1) * W, gt_ref[ds(u * W, W), :], channels)

    for m in range(1, chans):
        src = (n + chans - m) % chans
        arrive(slab(src, core, z), ("w", m))
        for q in range(1, clips):
            send(slab(src, core, z), slab(src, core, z), ("wz", m, q), {"clip": (z + q) % clips})
        send(slab(src, core, z), slab(src, core, z), ("ws", m, 0), sib_id)
    conv_early()
    for d in range(1, bands):
        place = x_place((b + bands - d) % bands, n)
        arrive(place, ("x", d, 0))
        for m in range(1, chans):
            send(place, place, ("x", d, m), {"chan": (n + m) % chans})
    back_early()
    for m in range(1, chans):
        place = g_place(b, (n + chans - m) % chans)
        arrive(place, ("g", 0, m))
        for j in range(1, width):
            send(place, place, ("g", j, m), {"band": (b + 2 * j) % bands})
        send(place, place, ("f", 0, m), sib_id)
    for j in range(1, width):
        place = g_place((b + bands - 2 * j) % bands, n)
        arrive(place, ("g", j, 0))
        send(place, place, ("f", j, 0), sib_id)

    keep_x.wait()
    widen_block(me)
    for d in range(1, bands):
        widen_block(((b + bands - d) % bands) * chans + n)
    for m in range(1, chans):
        src_n = (n + chans - m) % chans
        arrive(x_place(b, src_n), ("x", 0, m))
        widen_block(b * chans + src_n)
    for j in range(1, width):
        for m in range(1, chans):
            place = g_place((b + bands - 2 * j) % bands, (n + chans - m) % chans)
            arrive(place, ("g", j, m))
            send(place, place, ("f", j, m), sib_id)
    for d in range(1, bands):
        for m in range(1, chans):
            src_b, src_n = (b + bands - d) % bands, (n + chans - m) % chans
            arrive(x_place(src_b, src_n), ("x", d, m))
            widen_block(src_b * chans + src_n)
    send(xt_ref.at[pl.ds(cells - W, W), :], hx.at[0], ("hx", 0), nxt_id)
    send(gt_ref.at[pl.ds(cells - W, W), :], hg.at[0], ("hg", 0), nxt_id)
    send(xt_ref.at[pl.ds(0, W), :], hx.at[1], ("hx", 1), prv_id)
    send(gt_ref.at[pl.ds(0, W), :], hg.at[1], ("hg", 1), prv_id)
    for j in range(width):
        for m in range(chans):
            arrive(g_place((sib + bands - 2 * j) % bands, (n + chans - m) % chans), ("f", j, m))
    keep_g.wait()

    block = 2 * cells

    def tap_row(a):
        if total <= 8192:
            rows = jnp.dot(gs[...], dx[a * W:a * W + total, :], preferred_element_type=F32)
        else:
            held = acc_b.at[pl.ds(0, rows_o), pl.ds(0, 3 * rows_i)]
            held[...] = jnp.zeros((rows_o, 3 * rows_i), F32)

            @pl.loop(0, group // 2)
            def _(k):
                at = pl.ds(pl.multiple_of(k * block + a * W, 32), block)
                held[...] += jnp.dot(gs[:, ds(k * block, block)], dx[at, :], preferred_element_type=F32)

            rows = held[...]
        for t in range(3):
            share[3 * a + t] = rows[:, t * rows_i:(t + 1) * rows_i] * scale

    side = z // 2

    def spot(t, part, bb):
        return o_ref.at[t, part, :, ds(bb * rows_i, rows_i)]

    def spread(t, part, step):
        place = spot(t, part, b)
        for j in range(1, width):
            send(place, place, ("xo", t, step, j), {"band": (b + 2 * j) % bands})
        send(place, place, ("c", t, step, 0), sib_id)

    def give(t):
        for part in range(2):
            encode(coded, (t, part), share[t, part * half:(part + 1) * half, :])
        send(coded.at[t], got1.at[t], ("r1", t), near)

    def take(t):
        arrive(got1.at[t], ("r1", t))
        for part in range(2):
            share[t, part * half:(part + 1) * half, :] += decode(got1[t, part])
        encode(coded, (t, 0), share[t, ds((1 - side) * half, half), :])
        send(coded.at[t, 0], got2.at[t], ("r2", t), middle)

    def settle(t):
        arrive(got2.at[t], ("r2", t))
        encode(coded, (t, 1), share[t, ds(side * half, half), :] + decode(got2[t]))
        place = spot(t, side, b)
        place[...] = coded[t, 1]
        send(coded.at[t, 1], place, ("a1", t), middle)
        send(coded.at[t, 1], place, ("a2", t, 0), near)
        spread(t, side, 0)

    def share_back(t):
        place = spot(t, 1 - side, b)
        arrive(place, ("a1", t))
        send(place, place, ("a2", t, 1), near)
        spread(t, 1 - side, 1)

    def receive(t):
        for step, part in enumerate((side, 1 - side)):
            arrive(spot(t, part, b), ("a2", t, step))
            spread(t, part, step)

    def cross(t):
        for step, part in enumerate((side, 1 - side)):
            for j in range(1, width):
                place = spot(t, part, (b + bands - 2 * j) % bands)
                arrive(place, ("xo", t, step, j))
                send(place, place, ("c", t, step, j), sib_id)

    def finish(t):
        for step, part in enumerate((side, 1 - side)):
            for j in range(width):
                arrive(spot(t, part, (sib + bands - 2 * j) % bands), ("c", t, step, j))

    def bias_sum():
        ones = jnp.ones((8, block), BF16)
        dbs[...] = jnp.zeros((8, rows_o), F32)

        @pl.loop(0, group // 2)
        def _(k):
            dbs[...] += lax.dot_general(
                ones, gs[:, ds(k * block, block)], (((1,), (1,)), ((), ())), preferred_element_type=F32
            )

        for q in range(1, clips):
            send(dbs, dgot.at[q], ("d", q), {"clip": (z + q) % clips})

    def halos():
        for h in range(2):
            arrive(hx.at[h], ("hx", h))
            arrive(hg.at[h], ("hg", h))
            edge = me == (0 if h == 0 else group - 1)
            for src, dst in ((hx, xe), (hg, ge)):
                rows = src[h]
                rows = jnp.where(edge, jnp.zeros_like(rows), rows)
                for t, part in enumerate(sides(rows)):
                    dst[pl.ds(h * (cells + W), W), t * channels:(t + 1) * channels] = part

    def weights():
        for m in range(1, chans):
            src = (n + chans - m) % chans
            for q in range(1, clips):
                zz = (z + clips - q) % clips
                arrive(slab(src, core, zz), ("wz", m, q))
                send(slab(src, core, zz), slab(src, core, zz), ("ws", m, q), sib_id)
        for m in range(1, chans):
            src = (n + chans - m) % chans
            for q in range(clips):
                arrive(slab(src, 1 - core, (z + clips - q) % clips), ("ws", m, q))
        if not split:
            keep_w.wait()

    def back_out():
        @pl.loop(0, cells // 128)
        def _(t):
            back_ref[:, ds(t * 128, 128)] = acc_b[ds(t * 128, 128), :].T.astype(BF16)

    def matmuls():
        yield bias_sum()
        yield halos()
        first, size, count = (other, rows_o, stripe) if split else (0, channels, channels // 256)
        if split:
            yield conv_part(own, stripe, 0, cut, (0,), True, True)
            yield conv_part(own, stripe, cells - cut, cells, (2,), True, True)
            yield back_part(own, rows_o, 0, W, (0,), True)
            yield back_part(own, rows_o, cells - W, cells, (2,), True)
        yield weights()
        for lo, hi in ((0, cut), (cut, cells - cut), (cells - cut, cells)):
            yield conv_part(first, count, lo, hi, (0, 1, 2), False, True)
        for lo in (0, cells // 2):
            yield back_part(first, size, lo, lo + cells // 2, (0, 1, 2), split)
        yield back_out()

    gathered = list(started)

    def second_half(role):
        started.clear()
        work = matmuls()
        for a in range(3):
            tap_row(a)
            if not role:
                for t in range(3 * a, 3 * a + 3):
                    give(t)
        if role:
            for t in range(13):
                for step, lag in ((take, 0), (settle, 1), (share_back, 2), (cross, 4)):
                    if 0 <= t - lag < 9:
                        step(t - lag)
                next(work, None)
        else:
            for _ in range(3):
                next(work, None)
            for t in range(11):
                for step, lag in ((receive, 0), (cross, 2)):
                    if 0 <= t - lag < 9:
                        step(t - lag)
                next(work, None)
        for _ in work:
            pass
        for q in range(1, clips):
            arrive(dgot.at[q], ("d", q))
        sums = dbs[...]
        for q in range(1, clips):
            sums = sums + dgot[q]
        db_ref[...] = sums[:1] * scale
        for t in range(9):
            finish(t)
        for copy in started:
            copy.wait_send()

    @pl.when(inner)
    def _():
        second_half(True)

    @pl.when(jnp.logical_not(inner))
    def _():
        second_half(False)

    for copy in gathered:
        copy.wait_send()


def emit(*refs):
    sources, places, wide, sems = refs[:4], refs[4:8], refs[8], refs[9]
    copies = [pltpu.make_async_copy(src, dst, sems.at[i]) for i, (src, dst) in enumerate(zip(sources[1:], places[1:]))]
    for copy in copies:
        copy.start()
    taps, parts, rows, _ = sources[0].shape
    rows -= 16

    def out(t):
        return pltpu.make_async_copy(wide.at[t], places[0].at[t], sems.at[3 + t])

    @pl.loop(0, taps)
    def _(t):
        for part in range(parts):
            wide[t, part * rows:(part + 1) * rows, :] = decode(sources[0][t, part])
        out(t).start()

    @pl.loop(0, taps)
    def _(t):
        out(t).wait()

    for copy in copies:
        copy.wait()


VM = pl.BlockSpec(memory_space=pltpu.VMEM)


def local(frames, weight, bias, cotangent):
    channels, frame_count, cells = frames.shape
    clips, bands, chans = (lax.axis_size(a) for a in ("clip", "band", "chan"))
    group = bands * chans
    assert frame_count == 1 and cells % W == 0 and clips == 4
    total = cells * group
    scale = 1.0 / math.sqrt(frame_count * clips * total)
    rows_i, rows_o = channels // bands, channels // chans
    x = frames.reshape(channels, cells)
    g = cotangent.reshape(channels, cells)
    wt = jnp.transpose(weight, (1, 2, 0, 3)).reshape(9, rows_o, channels)
    half = rows_o // 2
    width = bands // 2
    copies = (chans - 1) * (1 + clips - 1 + clips) + 2 * width * chans + group + bands * chans + 4 + clips + 9 * (5 + 4 * width) + 8
    limit = (24 << 20) + (total + 2 * W) * 4 * rows_i * 2 + rows_o * total * 2 + rows_o * channels * 72
    shape = jax.ShapeDtypeStruct
    result = pltpu.VMEM if limit < (50 << 20) else shape
    grad, db, outputs, back = pl.pallas_call(
        functools.partial(kernel, (clips, bands, chans, rows_o, rows_i, cells, channels, scale)),
        out_shape=(
            result((9, 2, half + 16, channels), BF16),
            result((1, rows_o), F32),
            result((channels, cells), BF16),
            result((channels, cells), BF16),
        ),
        in_specs=[pl.BlockSpec(memory_space=pltpu.HBM)] * 4,
        out_specs=(VM,) * 4,
        scratch_shapes=[
            pltpu.VMEM((total, rows_i), BF16),
            pltpu.VMEM((rows_o, total), BF16),
            pltpu.VMEM((total + 2 * W, 3 * rows_i), BF16),
            pltpu.VMEM((cells + 2 * W, 3 * channels), BF16),
            pltpu.VMEM((cells + 2 * W, 3 * channels), BF16),
            pltpu.VMEM((9, channels, channels), BF16),
            pltpu.VMEM((rows_o, cells), F32),
            pltpu.VMEM((cells, channels), F32),
            pltpu.VMEM((9, rows_o, rows_i), F32),
            pltpu.VMEM((9, 2, half + 16, rows_i), BF16),
            pltpu.VMEM((9, 2, half + 16, rows_i), BF16),
            pltpu.VMEM((9, half + 16, rows_i), BF16),
            pltpu.VMEM((8, rows_o), F32),
            pltpu.VMEM((clips, 8, rows_o), F32),
            pltpu.VMEM((2, W, channels), BF16),
            pltpu.VMEM((2, W, channels), BF16),
            pltpu.VMEM((cells, channels), BF16),
            pltpu.VMEM((cells, channels), BF16),
            pltpu.VMEM((channels, cells), BF16),
            pltpu.VMEM((channels, cells), BF16),
            pltpu.VMEM((1, channels), F32),
            pltpu.SemaphoreType.DMA((2, copies)),
            pltpu.SemaphoreType.DMA((6,)),
        ],
        compiler_params=pltpu.CompilerParams(collective_id=0, has_side_effects=True, vmem_limit_bytes=min(67000000, limit)),
    )(*(pltpu.with_memory_space_constraint(v, pltpu.HBM) for v in (x, g, wt, bias[None, :])))
    results = (grad, db, outputs, back)
    grad, db, outputs, back = pl.pallas_call(
        emit,
        out_shape=(shape((9, rows_o, channels), F32),) + tuple(shape(r.shape, r.dtype) for r in results[1:]),
        in_specs=[VM] * 4,
        out_specs=(pl.BlockSpec(memory_space=pl.ANY),) * 4,
        scratch_shapes=[pltpu.VMEM((9, rows_o, channels), F32), pltpu.SemaphoreType.DMA((12,))],
        compiler_params=pltpu.CompilerParams(vmem_limit_bytes=16 << 20),
    )(*results)
    outputs = outputs.reshape(frames.shape)
    grad_frames = back.reshape(frames.shape)
    grad_weight = jnp.transpose(grad.reshape(3, 3, rows_o, channels), (2, 0, 1, 3))
    return outputs, grad_frames, grad_weight, db[0]


def solution(mesh):
    cells = P(None, "clip", ("band", "chan"))
    taps = P("chan", None, None, None)
    return jax.shard_map(
        local, mesh=mesh, in_specs=(cells, taps, P(), cells), out_specs=(cells, cells, taps, P("chan")), check_vma=False
    )
```

```python
import functools
import math

import jax
import jax.numpy as jnp
from jax import lax
from jax.experimental import pallas as pl
from jax.experimental.pallas import tpu as pltpu
from jax.sharding import PartitionSpec as P

W = 160
MESH = pl.DeviceIdType.MESH
F32 = jnp.float32
BF16 = jnp.bfloat16


def ds(start, size):
    return pl.ds(pl.multiple_of(start, size), size)


def remote(src, dst, send, recv, device):
    return pltpu.make_async_remote_copy(
        src_ref=src, dst_ref=dst, send_sem=send, recv_sem=recv, device_id=device, device_id_type=MESH
    )


def sides(rows):
    wide = rows.astype(F32)
    at = lax.broadcasted_iota(jnp.int32, wide.shape, 0)
    left = jnp.where(at == 0, 0.0, pltpu.roll(wide, 1, 0)).astype(BF16)
    right = jnp.where(at == W - 1, 0.0, pltpu.roll(wide, W - 1, 0)).astype(BF16)
    return left, rows, right


def encode(dst, at, value):
    rows, lanes = value.shape
    wide = value.reshape(rows // 16, 16, lanes)
    top = jnp.maximum(jnp.max(jnp.abs(wide), axis=0), 1e-35).astype(BF16)
    u = wide * (1.0 / top.astype(F32))
    power = u * u
    power = power * power
    power = power * power
    code = jnp.where(u < 0.0, -power, power).reshape(rows, lanes)
    dst[(*at, pl.ds(0, 16), slice(None))] = top
    dst[(*at, pl.ds(16, rows), slice(None))] = code.astype(BF16)


def decode(block):
    rows, lanes = block.shape
    top = block[:16].astype(F32)
    code = block[16:].astype(F32)
    root = jnp.exp(jnp.log(jnp.abs(code)) * 0.125)
    root = jnp.where(code > 0.0, root, jnp.where(code < 0.0, -root, 0.0))
    return (root.reshape(rows // 16 - 1, 16, lanes) * top).reshape(rows - 16, lanes)


def kernel(
    dims, x_in, g_in, w_ref, bias_in, o_ref, db_ref, out_ref, back_ref,
    xs, gs, dx, xe, ge, kern, acc_f, acc_o, acc_b, share, coded, final, got1, got2, dbs, dgot, hx, hg, xt_ref, gt_ref, x_ref, g_ref, bias_ref, sems, regs,
):
    clips, bands, chans, rows_o, rows_i, cells, channels, scale = dims
    group = bands * chans
    half = rows_o // 2
    lanes = channels // clips
    width = bands // 2
    units = cells // W
    split = chans == 2 and rows_o % 256 == 0
    cut = -(-W // 128) * 128
    total = cells * group
    z, b, n = lax.axis_index("clip"), lax.axis_index("band"), lax.axis_index("chan")
    me = b * chans + n
    core = b % 2
    sib = b + 1 - 2 * core
    sib_id = {"band": sib}
    nxt, prv = (me + 1) % group, (me + group - 1) % group
    nxt_id = {"band": nxt // chans, "chan": nxt % chans}
    prv_id = {"band": prv // chans, "chan": prv % chans}
    z0 = z % 2
    inner = (z + 1) // 2 == 1
    near, middle = {"clip": z + 1 - 2 * z0}, {"clip": clips - 1 - z}

    loads = [
        pltpu.make_async_copy(src, dst, regs.at[3 + i])
        for i, (src, dst) in enumerate(((x_in, x_ref), (g_in, g_ref), (bias_in, bias_ref)))
    ]
    for load in loads:
        load.start()
    barrier = pltpu.get_barrier_semaphore()
    targets = [{"clip": (z + k) % clips} for k in range(1, clips)]
    for k in range(1, group):
        to = (me + k) % group
        targets.append({"band": to // chans, "chan": to % chans})
    for target in targets:
        pl.semaphore_signal(barrier, inc=1, device_id=target, device_id_type=MESH)

    def turn(src, dst):
        @pl.loop(0, cells // 128)
        def _(t):
            dst[ds(t * 128, 128), :] = src[:, ds(t * 128, 128)].astype(F32).T.astype(BF16)

    loads[0].wait()
    turn(x_ref, xt_ref)
    loads[1].wait()
    loads[2].wait()
    pl.semaphore_wait(barrier, len(targets))

    started = []
    names = {}

    def pair(key):
        if key not in names:
            names[key] = len(names)
        return sems.at[0, names[key]], sems.at[1, names[key]]

    def send(src, dst, key, device):
        s, r = pair(key)
        copy = remote(src, dst, s, r, device)
        copy.start()
        started.append(copy)

    def arrive(dst, key):
        s, r = pair(key)
        remote(dst, dst, s, r, sib_id).wait_recv()

    def slab(src_n, part, zz):
        return kern.at[pl.ds(0, 6), ds((2 * src_n + part) * half, half), ds(zz * lanes, lanes)]

    def late(src_n, part):
        return kern.at[pl.ds(6, 3), ds((2 * src_n + part) * half, half), :]

    keep_w = pltpu.make_async_copy(w_ref, kern.at[:, ds(n * rows_o, rows_o), :], regs.at[0])
    keep_x = pltpu.make_async_copy(xt_ref.at[:, ds(b * rows_i, rows_i)], xs.at[ds(me * cells, cells), :], regs.at[1])
    keep_g = pltpu.make_async_copy(g_ref.at[ds(n * rows_o, rows_o), :], gs.at[:, ds(me * cells, cells)], regs.at[2])

    def x_place(src_b, src_n):
        return xs.at[ds((src_b * chans + src_n) * cells, cells), :]

    def g_place(src_b, src_n):
        return gs.at[:, ds((src_b * chans + src_n) * cells, cells)]

    for m in range(1, chans):
        send(w_ref.at[pl.ds(0, 6), ds(core * half, half), ds(z * lanes, lanes)], slab(n, core, z), ("w", m), {"chan": (n + m) % chans})
    for d in range(1, bands):
        to_b = (b + d) % bands
        send(xt_ref.at[:, ds(to_b * rows_i, rows_i)], x_place(b, n), ("x", d, 0), {"band": to_b})
    for m in range(1, chans):
        to_n = (n + m) % chans
        send(g_ref.at[ds(to_n * rows_o, rows_o), :], g_place(b, n), ("g", 0, m), {"chan": to_n})
        send(xt_ref.at[:, ds(b * rows_i, rows_i)], x_place(b, n), ("x", 0, m), {"chan": to_n})
    own_g = g_ref.at[ds(n * rows_o, rows_o), :]
    for j in range(1, width):
        send(own_g, g_place(b, n), ("g", j, 0), {"band": (b + 2 * j) % bands})
    send(own_g, g_place(b, n), ("f", 0, 0), sib_id)
    keep_x.start()
    keep_g.start()
    keep_w.start()

    def widen(dst, to, rows, size):
        for t, part in enumerate(sides(rows)):
            dst[ds(to, W), t * size:(t + 1) * size] = part

    def widen_block(src):
        @pl.loop(0, units)
        def _(u):
            at = src * cells + u * W
            widen(dx, at + W, xs[ds(at, W), :], rows_i)

    def conv_part(acc, start, count, lo, hi, taps, seed, last):
        @pl.loop(0, count)
        def _(t):
            at, rows = ds(t * 256, 256), ds(start + t * 256, 256)
            if seed:
                part = acc[at, lo:hi]
            else:
                column = jnp.broadcast_to(bias_ref[:, rows], (8, 256)).T[:, :1]
                part = jnp.zeros((256, hi - lo), F32) + column
            for a in taps:
                for s in range(3):
                    part += lax.dot_general(
                        kern[3 * a + s, rows, :], xe[a * W + lo:a * W + hi, s * channels:(s + 1) * channels],
                        (((1,), (1,)), ((), ())), preferred_element_type=F32,
                    )
            if last:
                out_ref[rows, lo:hi] = part.astype(BF16)
            else:
                acc[at, lo:hi] = part

    def back_part(start, size, lo, hi, rows, seed):
        part = acc_b[lo:hi, :] if seed else jnp.zeros((hi - lo, channels), F32)
        for c in rows:
            for s in range(3):
                cols = pl.ds(pl.multiple_of((2 - s) * channels + start, 128), size)
                part += jnp.dot(
                    ge[c * W + lo:c * W + hi, cols], kern[3 * (2 - c) + s, pl.ds(pl.multiple_of(start, 16), size), :],
                    preferred_element_type=F32,
                )
        acc_b[lo:hi, :] = part

    own, other, stripe = n * rows_o, (1 - n) * rows_o, rows_o // 256

    def conv_early():
        if split:
            keep_w.wait()
            conv_part(acc_f, own, stripe, 0, cut, (1, 2), False, False)
            conv_part(acc_f, own, stripe, cut, cells - cut, (0, 1, 2), False, True)
            conv_part(acc_f, own, stripe, cells - cut, cells, (0, 1), False, False)

    def back_early():
        if split:
            back_part(own, rows_o, 0, W, (1, 2), False)
            back_part(own, rows_o, W, cells - W, (0, 1, 2), False)
            back_part(own, rows_o, cells - W, cells, (0, 1), False)

    turn(g_ref, gt_ref)
    dx[pl.ds(0, W), :] = jnp.zeros((W, 3 * rows_i), BF16)
    dx[pl.ds(total + W, W), :] = jnp.zeros((W, 3 * rows_i), BF16)

    @pl.loop(0, units)
    def _(u):
        widen(xe, (u + 1) * W, xt_ref[ds(u * W, W), :], channels)
        widen(ge, (u + 1) * W, gt_ref[ds(u * W, W), :], channels)

    for m in range(1, chans):
        src = (n + chans - m) % chans
        arrive(slab(src, core, z), ("w", m))
        for q in range(1, clips):
            send(slab(src, core, z), slab(src, core, z), ("wz", m, q), {"clip": (z + q) % clips})
        send(slab(src, core, z), slab(src, core, z), ("ws", m, 0), sib_id)
    conv_early()
    for d in range(1, bands):
        place = x_place((b + bands - d) % bands, n)
        arrive(place, ("x", d, 0))
        for m in range(1, chans):
            send(place, place, ("x", d, m), {"chan": (n + m) % chans})
    back_early()
    for m in range(1, chans):
        place = g_place(b, (n + chans - m) % chans)
        arrive(place, ("g", 0, m))
        for j in range(1, width):
            send(place, place, ("g", j, m), {"band": (b + 2 * j) % bands})
        send(place, place, ("f", 0, m), sib_id)
    for j in range(1, width):
        place = g_place((b + bands - 2 * j) % bands, n)
        arrive(place, ("g", j, 0))
        send(place, place, ("f", j, 0), sib_id)

    keep_x.wait()
    widen_block(me)
    for d in range(1, bands):
        widen_block(((b + bands - d) % bands) * chans + n)
    for m in range(1, chans):
        src_n = (n + chans - m) % chans
        arrive(x_place(b, src_n), ("x", 0, m))
        widen_block(b * chans + src_n)
    for j in range(1, width):
        for m in range(1, chans):
            place = g_place((b + bands - 2 * j) % bands, (n + chans - m) % chans)
            arrive(place, ("g", j, m))
            send(place, place, ("f", j, m), sib_id)
    for d in range(1, bands):
        for m in range(1, chans):
            src_b, src_n = (b + bands - d) % bands, (n + chans - m) % chans
            arrive(x_place(src_b, src_n), ("x", d, m))
            widen_block(src_b * chans + src_n)
    send(xt_ref.at[pl.ds(cells - W, W), :], hx.at[0], ("hx", 0), nxt_id)
    send(gt_ref.at[pl.ds(cells - W, W), :], hg.at[0], ("hg", 0), nxt_id)
    send(xt_ref.at[pl.ds(0, W), :], hx.at[1], ("hx", 1), prv_id)
    send(gt_ref.at[pl.ds(0, W), :], hg.at[1], ("hg", 1), prv_id)
    for m in range(1, chans):
        send(w_ref.at[pl.ds(6, 3), ds(core * half, half), :], late(n, core), ("wl", m), {"chan": (n + m) % chans})
    for j in range(width):
        for m in range(chans):
            arrive(g_place((sib + bands - 2 * j) % bands, (n + chans - m) % chans), ("f", j, m))
    keep_g.wait()

    block = 2 * cells

    def tap_row(a):
        if total <= 8192:
            rows = jnp.dot(gs[...], dx[a * W:a * W + total, :], preferred_element_type=F32)
        else:
            held = acc_b.at[pl.ds(0, rows_o), pl.ds(0, 3 * rows_i)]
            held[...] = jnp.zeros((rows_o, 3 * rows_i), F32)

            @pl.loop(0, group // 2)
            def _(k):
                at = pl.ds(pl.multiple_of(k * block + a * W, 32), block)
                held[...] += jnp.dot(gs[:, ds(k * block, block)], dx[at, :], preferred_element_type=F32)

            rows = held[...]
        for t in range(3):
            share[3 * a + t] = rows[:, t * rows_i:(t + 1) * rows_i] * scale

    def spot(t, bb):
        return o_ref.at[t, :, :, ds(bb * rows_i, rows_i)]

    def spread(t):
        place = spot(t, b)
        for j in range(1, width):
            send(place, place, ("xo", t, j), {"band": (b + 2 * j) % bands})
        send(place, place, ("c", t, 0), sib_id)

    def give(t):
        for part in range(2):
            encode(coded, (t, part), share[t, part * half:(part + 1) * half, :])
        send(coded.at[t], got1.at[t], ("r1", t), near)

    def take(t):
        arrive(got1.at[t], ("r1", t))
        for part in range(2):
            encode(coded, (t, part), share[t, part * half:(part + 1) * half, :] + decode(got1[t, part]))
        send(coded.at[t], got2.at[t], ("r2", t), middle)

    def settle(t):
        arrive(got2.at[t], ("r2", t))
        for part in range(2):
            encode(final, (t, part), decode(coded[t, part]) + decode(got2[t, part]))
        place = spot(t, b)
        send(final.at[t], place, ("a2", t), near)
        for j in range(1, width):
            send(final.at[t], place, ("xo", t, j), {"band": (b + 2 * j) % bands})
        send(final.at[t], place, ("c", t, 0), sib_id)
        place[...] = final[t]

    def receive(t):
        arrive(spot(t, b), ("a2", t))
        spread(t)

    def cross(t):
        for j in range(1, width):
            place = spot(t, (b + bands - 2 * j) % bands)
            arrive(place, ("xo", t, j))
            send(place, place, ("c", t, j), sib_id)

    def finish(t):
        for j in range(width):
            arrive(spot(t, (sib + bands - 2 * j) % bands), ("c", t, j))

    def bias_sum():
        ones = jnp.ones((8, block), BF16)
        dbs[...] = jnp.zeros((8, rows_o), F32)

        @pl.loop(0, group // 2)
        def _(k):
            dbs[...] += lax.dot_general(
                ones, gs[:, ds(k * block, block)], (((1,), (1,)), ((), ())), preferred_element_type=F32
            )

        for q in range(1, clips):
            send(dbs, dgot.at[q], ("d", q), {"clip": (z + q) % clips})

    def halos():
        for h in range(2):
            arrive(hx.at[h], ("hx", h))
            arrive(hg.at[h], ("hg", h))
            edge = me == (0 if h == 0 else group - 1)
            for src, dst in ((hx, xe), (hg, ge)):
                rows = src[h]
                rows = jnp.where(edge, jnp.zeros_like(rows), rows)
                for t, part in enumerate(sides(rows)):
                    dst[pl.ds(h * (cells + W), W), t * channels:(t + 1) * channels] = part

    def weights():
        for m in range(1, chans):
            src = (n + chans - m) % chans
            for q in range(1, clips):
                zz = (z + clips - q) % clips
                arrive(slab(src, core, zz), ("wz", m, q))
                send(slab(src, core, zz), slab(src, core, zz), ("ws", m, q), sib_id)
        for m in range(1, chans):
            src = (n + chans - m) % chans
            for q in range(clips):
                arrive(slab(src, 1 - core, (z + clips - q) % clips), ("ws", m, q))
        if not split:
            keep_w.wait()

    def weights_late():
        for m in range(1, chans):
            src = (n + chans - m) % chans
            arrive(late(src, core), ("wl", m))
            send(late(src, core), late(src, core), ("wls", m), sib_id)

    def weights_there():
        for m in range(1, chans):
            arrive(late((n + chans - m) % chans, 1 - core), ("wls", m))

    def back_out():
        @pl.loop(0, cells // 128)
        def _(t):
            back_ref[:, ds(t * 128, 128)] = acc_b[ds(t * 128, 128), :].T.astype(BF16)

    def back_rows(row):
        for lo in (0, cells // 2):
            yield back_part(other, rows_o, lo, lo + cells // 2, (2 - row,), True)

    def matmuls():
        yield bias_sum()
        if not split:
            halos()
            weights()
            weights_late()
            weights_there()
            for lo, hi in ((0, cut), (cut, cells - cut), (cells - cut, cells)):
                yield conv_part(acc_f, 0, channels // 256, lo, hi, (0, 1, 2), False, True)
            for lo in (0, cells // 2):
                yield back_part(0, channels, lo, lo + cells // 2, (0, 1, 2), False)
            yield back_out()
            return
        yield weights()
        yield conv_part(acc_o, other, stripe, 0, cut, (1,), False, False)
        yield conv_part(acc_o, other, stripe, cut, cells, (1,), False, False)
        yield from back_rows(1)
        yield conv_part(acc_o, other, stripe, cut, cells, (0,), True, False)
        yield halos()
        yield conv_part(acc_f, own, stripe, 0, cut, (0,), True, True)
        yield conv_part(acc_f, own, stripe, cells - cut, cells, (2,), True, True)
        yield back_part(own, rows_o, 0, W, (0,), True)
        yield back_part(own, rows_o, cells - W, cells, (2,), True)
        yield conv_part(acc_o, other, stripe, 0, cut, (0,), True, False)
        yield from back_rows(0)
        weights_late()
        yield weights_there()
        yield conv_part(acc_o, other, stripe, 0, cut, (2,), True, True)
        yield conv_part(acc_o, other, stripe, cut, cells, (2,), True, True)
        yield from back_rows(2)
        yield back_out()

    gathered = list(started)

    def second_half(role):
        started.clear()
        work = matmuls()
        for a in range(3):
            tap_row(a)
            if not role:
                for t in range(3 * a, 3 * a + 3):
                    give(t)
        if role:
            for t in range(12):
                for step, lag in ((take, 0), (settle, 1), (cross, 3)):
                    if 0 <= t - lag < 9:
                        step(t - lag)
                next(work, None)
        else:
            for _ in range(6):
                next(work, None)
            for t in range(11):
                for step, lag in ((receive, 0), (cross, 2)):
                    if 0 <= t - lag < 9:
                        step(t - lag)
                next(work, None)
        for _ in work:
            pass
        for q in range(1, clips):
            arrive(dgot.at[q], ("d", q))
        sums = dbs[...]
        for q in range(1, clips):
            sums = sums + dgot[q]
        db_ref[...] = sums[:1] * scale
        for t in range(9):
            finish(t)
        for copy in started:
            copy.wait_send()

    @pl.when(inner)
    def _():
        second_half(True)

    @pl.when(jnp.logical_not(inner))
    def _():
        second_half(False)

    for copy in gathered:
        copy.wait_send()


def emit(*refs):
    sources, places, wide, sems = refs[:4], refs[4:8], refs[8], refs[9]
    copies = [pltpu.make_async_copy(src, dst, sems.at[i]) for i, (src, dst) in enumerate(zip(sources[1:], places[1:]))]
    for copy in copies:
        copy.start()
    taps, parts, rows, _ = sources[0].shape
    rows -= 16

    def out(t):
        return pltpu.make_async_copy(wide.at[t], places[0].at[t], sems.at[3 + t])

    @pl.loop(0, taps)
    def _(t):
        for part in range(parts):
            wide[t, part * rows:(part + 1) * rows, :] = decode(sources[0][t, part])
        out(t).start()

    @pl.loop(0, taps)
    def _(t):
        out(t).wait()

    for copy in copies:
        copy.wait()


VM = pl.BlockSpec(memory_space=pltpu.VMEM)


def local(frames, weight, bias, cotangent):
    channels, frame_count, cells = frames.shape
    clips, bands, chans = (lax.axis_size(a) for a in ("clip", "band", "chan"))
    group = bands * chans
    assert frame_count == 1 and cells % W == 0 and clips == 4
    total = cells * group
    scale = 1.0 / math.sqrt(frame_count * clips * total)
    rows_i, rows_o = channels // bands, channels // chans
    x = frames.reshape(channels, cells)
    g = cotangent.reshape(channels, cells)
    wt = jnp.transpose(weight, (1, 2, 0, 3)).reshape(9, rows_o, channels)
    half = rows_o // 2
    width = bands // 2
    copies = (chans - 1) * (1 + clips - 1 + clips) + 2 * width * chans + group + bands * chans + 4 + clips + 9 * (5 + 4 * width) + 8 + 4 * chans
    limit = (24 << 20) + (total + 2 * W) * 4 * rows_i * 2 + rows_o * total * 2 + rows_o * channels * 72
    shape = jax.ShapeDtypeStruct
    result = pltpu.VMEM if limit < (50 << 20) else shape
    grad, db, outputs, back = pl.pallas_call(
        functools.partial(kernel, (clips, bands, chans, rows_o, rows_i, cells, channels, scale)),
        out_shape=(
            result((9, 2, half + 16, channels), BF16),
            result((1, rows_o), F32),
            result((channels, cells), BF16),
            result((channels, cells), BF16),
        ),
        in_specs=[pl.BlockSpec(memory_space=pltpu.HBM)] * 4,
        out_specs=(VM,) * 4,
        scratch_shapes=[
            pltpu.VMEM((total, rows_i), BF16),
            pltpu.VMEM((rows_o, total), BF16),
            pltpu.VMEM((total + 2 * W, 3 * rows_i), BF16),
            pltpu.VMEM((cells + 2 * W, 3 * channels), BF16),
            pltpu.VMEM((cells + 2 * W, 3 * channels), BF16),
            pltpu.VMEM((9, channels, channels), BF16),
            pltpu.VMEM((rows_o, cells), F32),
            pltpu.VMEM((rows_o, cells), F32),
            pltpu.VMEM((cells, channels), F32),
            pltpu.VMEM((9, rows_o, rows_i), F32),
            pltpu.VMEM((9, 2, half + 16, rows_i), BF16),
            pltpu.VMEM((9, 2, half + 16, rows_i), BF16),
            pltpu.VMEM((9, 2, half + 16, rows_i), BF16),
            pltpu.VMEM((9, 2, half + 16, rows_i), BF16),
            pltpu.VMEM((8, rows_o), F32),
            pltpu.VMEM((clips, 8, rows_o), F32),
            pltpu.VMEM((2, W, channels), BF16),
            pltpu.VMEM((2, W, channels), BF16),
            pltpu.VMEM((cells, channels), BF16),
            pltpu.VMEM((cells, channels), BF16),
            pltpu.VMEM((channels, cells), BF16),
            pltpu.VMEM((channels, cells), BF16),
            pltpu.VMEM((1, channels), F32),
            pltpu.SemaphoreType.DMA((2, copies)),
            pltpu.SemaphoreType.DMA((6,)),
        ],
        compiler_params=pltpu.CompilerParams(collective_id=0, has_side_effects=True, vmem_limit_bytes=min(67000000, limit)),
    )(*(pltpu.with_memory_space_constraint(v, pltpu.HBM) for v in (x, g, wt, bias[None, :])))
    results = (grad, db, outputs, back)
    grad, db, outputs, back = pl.pallas_call(
        emit,
        out_shape=(shape((9, rows_o, channels), F32),) + tuple(shape(r.shape, r.dtype) for r in results[1:]),
        in_specs=[VM] * 4,
        out_specs=(pl.BlockSpec(memory_space=pl.ANY),) * 4,
        scratch_shapes=[pltpu.VMEM((9, rows_o, channels), F32), pltpu.SemaphoreType.DMA((12,))],
        compiler_params=pltpu.CompilerParams(vmem_limit_bytes=16 << 20),
    )(*results)
    outputs = outputs.reshape(frames.shape)
    grad_frames = back.reshape(frames.shape)
    grad_weight = jnp.transpose(grad.reshape(3, 3, rows_o, channels), (2, 0, 1, 3))
    return outputs, grad_frames, grad_weight, db[0]


def solution(mesh):
    cells = P(None, "clip", ("band", "chan"))
    taps = P("chan", None, None, None)
    return jax.shard_map(
        local, mesh=mesh, in_specs=(cells, taps, P(), cells), out_specs=(cells, cells, taps, P("chan")), check_vma=False
    )
```
